512 devices in a mesh: seq: 128 (over y, z, x_lo), batch: 4 (over x_hi, core).
Axes of the slice: x: 4 (x_hi: 2, x_lo: 2; x = x_hi * 2 + x_lo), y: 4, z: 16, core: 2. Of those that a mesh axis runs over, the one named last changes fastest.
Arguments:
- tokens: bfloat16 [4, 262144, 256], P('batch', 'seq'), may hold values from -6 to 6
- cotangent: bfloat16 [4, 262144, 256], P('batch', 'seq'), may hold values from -3 to 3
- first_factor: bfloat16 [512, 512, 512], P('seq', 'batch'), may hold values from -0.25 to 0.25
- second_factor: bfloat16 [512, 512, 512], P('seq', 'batch'), may hold values from -0.25 to 0.25
- gate_source: int32 [256], replicated, may hold values from 0 to 255
- alternate: int32 [512], replicated, may hold values from 0 to 511, each once
Outputs:
- grad_tokens: bfloat16 [4, 262144, 256], P('batch', 'seq')
- grad_first: bfloat16 [512, 512, 512], P('seq', 'batch')
- grad_second: bfloat16 [512, 512, 512], P('seq', 'batch')
The draws below stay inside these ranges and needn't reach their ends.
Inputs may be any that keep to these rules, and one draw needn't show every extreme that they name: `alternate`: a permutation: each of 0 to 511 once.
All inputs are finite; a program needn't handle non-finite values.
Results may differ from the reference program's by a relative error of at most 0.012.
Values may be sent and summed in bfloat16 or wider, within the bound.
A program may use at most 64 MiB of HBM per device.

```python
import jax
import jax.numpy as jnp
from jax import lax

BLOCK_ORDER = 512
CHANNELS = 256
BLOCKS = 512
SEQ_LEN = 262144
SEQUENCES = 4


def plant(entries, key, least, top_value):
    dims = entries.shape
    place = [jax.random.randint(jax.random.fold_in(key, axis), (), 0, dims[axis]) for axis in range(len(dims))]
    entries = entries.at[tuple(place)].set(least)
    longest = dims.index(max(dims))
    place[longest] = (place[longest] + 1) % dims[longest]
    return entries.at[tuple(place)].set(top_value)


def level_of(own_key, dims, split, smallest, largest):
    gain, own = 1.0, jax.random.fold_in(own_key, 6)
    for position, blocks in split:
        heights = jnp.exp(jax.random.uniform(jax.random.fold_in(own, position), (blocks,), jnp.float32, smallest / len(split), largest / len(split)))
        gain = gain * jnp.repeat(heights, dims[position] // blocks).reshape([-1 if axis == position else 1 for axis in range(len(dims))])
    return gain


def centred(key, extent, width, limit, split=(), kind=jnp.bfloat16):
    array = jax.random.normal(key, extent, jnp.float32) * width
    if len(split) > 0:
        array = level_of(key, extent, split, -0.22, 0.18) * array
    return jnp.clip(array, min=-limit, max=limit).astype(kind)


def setup_inputs(seed: int = 0) -> dict:
    key_of = jax.random.split(jax.random.key(seed), 7)
    tokens = centred(key_of[0], (SEQUENCES, SEQ_LEN, CHANNELS), 1.0, 6.0, ((0, 4), (1, 128)))
    cotangent = centred(key_of[1], (SEQUENCES, SEQ_LEN, CHANNELS), 0.5, 3.0, ((0, 4), (1, 128)))
    first_factor = centred(key_of[2], (BLOCKS, BLOCK_ORDER, BLOCK_ORDER), BLOCK_ORDER ** -0.5, 0.25, ((0, 128), (1, 4)))
    second_factor = centred(key_of[3], (BLOCK_ORDER, BLOCKS, BLOCKS), BLOCKS ** -0.5, 0.25, ((0, 128), (1, 4)))
    gate_source = plant(jax.random.randint(key_of[4], (CHANNELS,), 0, CHANNELS), jax.random.fold_in(key_of[4], 1), 0, CHANNELS - 1).astype(jnp.int32)
    alternate = jax.random.permutation(key_of[5], BLOCK_ORDER).astype(jnp.int32)
    return dict(tokens=tokens, cotangent=cotangent, first_factor=first_factor, second_factor=second_factor, gate_source=gate_source, alternate=alternate)


def reference(tokens, cotangent, first_factor, second_factor, gate_source, alternate):
    first_wide = first_factor.astype(jnp.float32)
    second_wide = second_factor.astype(jnp.float32)
    positions = jnp.arange(BLOCK_ORDER, dtype=jnp.int32)
    inverse = jnp.zeros((BLOCK_ORDER,), jnp.int32).at[alternate].set(positions)
    grad_one = jnp.zeros((BLOCKS, BLOCK_ORDER, BLOCK_ORDER), jnp.float32)
    grad_two = jnp.zeros((BLOCK_ORDER, BLOCKS, BLOCKS), jnp.float32)
    results = []
    for seq_index in range(SEQUENCES):
        inputs = tokens[seq_index]
        gate = jax.nn.sigmoid(inputs[:, gate_source].astype(jnp.float32))
        blocked = inputs.reshape(BLOCKS, BLOCK_ORDER, CHANNELS).astype(jnp.float32)
        mixed = jnp.einsum("ikj,ijc->ikc", first_wide, blocked).astype(jnp.bfloat16)
        regrouped = mixed[:, alternate, :]
        regrouped_wide = regrouped.astype(jnp.float32)
        z_out = jnp.einsum("jmi,ijc->jmc", second_wide, regrouped_wide).reshape(SEQ_LEN, CHANNELS)
        cot = cotangent[seq_index].astype(jnp.float32)
        dz_out = (cot * gate).astype(jnp.bfloat16)
        dgate = cot * z_out * gate * (1.0 - gate)
        dz_wide = dz_out.reshape(BLOCK_ORDER, BLOCKS, CHANNELS).astype(jnp.float32)
        part_two = jnp.einsum("jmc,ijc->jmi", dz_wide, regrouped_wide).astype(jnp.bfloat16)
        grad_two = grad_two + lax.optimization_barrier(part_two).astype(jnp.float32)
        dregrouped = jnp.einsum("jmi,jmc->ijc", second_wide, dz_wide).astype(jnp.bfloat16)
        dmixed = dregrouped[:, inverse, :].astype(jnp.float32)
        part_one = jnp.einsum("ikc,ijc->ikj", dmixed, blocked).astype(jnp.bfloat16)
        grad_one = grad_one + lax.optimization_barrier(part_one).astype(jnp.float32)
        dmix_in = jnp.einsum("ikj,ikc->ijc", first_wide, dmixed).reshape(SEQ_LEN, CHANNELS)
        spread = jax.ops.segment_sum(dgate.T, gate_source, num_segments=CHANNELS).T
        results.append((dmix_in + spread).astype(jnp.bfloat16))
    return jnp.stack(results), grad_one.astype(jnp.bfloat16), grad_two.astype(jnp.bfloat16)
```

```python
import functools

import jax
import jax.numpy as jnp
from jax import lax
from jax.experimental import pallas as pl
from jax.experimental.pallas import tpu as pltpu
from jax.sharding import PartitionSpec as P

MESH = pl.DeviceIdType.MESH
BF = jnp.bfloat16
F32 = jnp.float32


def push(src, dst, send_sem, recv_sem, device):
    return pltpu.make_async_remote_copy(
        src_ref=src,
        dst_ref=dst,
        send_sem=send_sem,
        recv_sem=recv_sem,
        device_id=device,
        device_id_type=MESH,
    )


def dot(a, b, da=1, db=0):
    return lax.dot_general(a, b, (((da,), (db,)), ((), ())), preferred_element_type=F32)


def kernel(
    n,
    tokens,
    cot,
    first,
    second,
    source,
    alt,
    grad_tokens,
    grad_first,
    grad_second,
    full,
    select,
    gate,
    dz,
    spread,
    pick,
    pick_t,
    mix4,
    mix8,
    column,
    send1,
    land1,
    send2,
    land2,
    regrouped,
    dcolumn,
    dmixed,
    term,
    near,
    staged,
    away,
    ag_send,
    ag_recv,
    a2a_send,
    a2a_recv,
    rs_send,
    rs_recv,
):
    order = alt.shape[1]
    width = tokens.shape[1]
    nb = first.shape[0]
    part = first.shape[1]
    group = min(16, n)
    groups = n // group
    span = group * nb
    s = lax.axis_index("seq")
    b = lax.axis_index("batch")
    other = b + 1 - 2 * lax.rem(b, 2)
    far = lax.rem(b + 2, 4)
    other_far = lax.rem(other + 2, 4)
    shards = (first, second)

    barrier = pltpu.get_barrier_semaphore()
    for peer in (other, far):
        pl.semaphore_signal(barrier, inc=1, device_id={"batch": peer}, device_id_type=MESH)

    def greet(r, carry):
        pl.semaphore_signal(
            barrier, inc=1, device_id={"seq": lax.rem(s + r, n)}, device_id_type=MESH
        )
        return carry

    lax.fori_loop(1, n, greet, 0)

    row = lax.broadcasted_iota(jnp.int32, (order, order), 0)
    hit = (row == alt[...]).astype(F32)
    pick_t[...] = hit.astype(BF)
    pick[...] = hit.T.astype(BF)
    select[...] = (
        lax.broadcasted_iota(jnp.int32, (width, width), 0) == source[...]
    ).astype(F32).astype(BF)
    rows4 = group * 8
    r4 = lax.broadcasted_iota(jnp.int32, (rows4, rows4), 0)
    c4 = lax.broadcasted_iota(jnp.int32, (rows4, rows4), 1)
    want = ((r4 // 4) % 2) * span + (r4 // 8) * 4 + r4 % 4
    mix4[...] = (want == c4).astype(F32).astype(BF)
    rows8 = group * 16
    r8 = lax.broadcasted_iota(jnp.int32, (rows8, rows8), 0)
    c8 = lax.broadcasted_iota(jnp.int32, (rows8, rows8), 1)
    want = (r8 % 4) * span + ((r8 // 8) % group) * 4 + (r8 // rows4) * 2 + (r8 // 4) % 2
    mix8[...] = (want == c8).astype(F32).astype(BF)
    for f in range(2):
        full[f, :, b] = shards[f][...]

    pl.semaphore_wait(barrier, n + 1)

    def to_far(f, i):
        return push(
            shards[f].at[i], full.at[f, i, b], ag_send.at[f, i, 0], ag_recv.at[f, i, 0], {"batch": far}
        )

    def to_other(f, i):
        return push(
            shards[f].at[i], full.at[f, i, b], ag_send.at[f, i, 1], ag_recv.at[f, i, 1], {"batch": other}
        )

    def onward(f, i):
        return push(
            full.at[f, i, far], full.at[f, i, far], ag_send.at[f, i, 2], ag_recv.at[f, i, 2], {"batch": other}
        )

    for f in range(2):
        for i in range(nb):
            to_far(f, i).start()
            to_other(f, i).start()

    def block(f, i):
        return full[f, i].reshape(order, order)

    def exchange(k, h, buf, land):
        def go(r, carry):
            p = lax.rem(s + r, n)
            push(
                buf.at[h, p], land.at[h, s], a2a_send.at[k, h], a2a_recv.at[k, h], {"seq": p}
            ).start()
            return carry

        lax.fori_loop(1, n, go, 0)
        land[h, s] = buf[h, s]

    def exchanged(k, h, buf, land):
        rest = pl.ds(0, n - 1)
        return push(
            buf.at[h, rest],
            land.at[h, rest],
            a2a_send.at[k, h],
            a2a_recv.at[k, h],
            {"seq": lax.rem(s + 1, n)},
        )

    for h in range(2):
        for i in (2 * h, 2 * h + 1):
            to_far(0, i).wait_recv()
            onward(0, i).start()
        for i in (2 * h, 2 * h + 1):
            to_other(0, i).wait_recv()
            onward(0, i).wait_recv()

            def apply(i2, carry, h=h):
                i = 2 * h + i2
                x = tokens[pl.ds(pl.multiple_of(i * order, order), order), :]
                mixed = dot(block(0, i), x).astype(BF)
                regrouped[i2] = dot(pick[...], mixed).astype(BF)
                return carry

            apply(i - 2 * h, 0)

        def pack(g, carry, h=h):
            at = pl.ds(pl.multiple_of(g * span, span), span)
            stack = jnp.concatenate([regrouped[0, at], regrouped[1, at]], axis=0)
            out = dot(mix4[...], stack)
            send1[h, pl.ds(g * group, group)] = out.reshape(group, 8, width).astype(BF)
            return carry

        lax.fori_loop(0, groups, pack, 0)
        exchange(0, h, send1, land1)

    def gating(q, carry):
        at = pl.ds(pl.multiple_of(q * order, order), order)
        g = jax.nn.sigmoid(dot(tokens[at, :], select[...]))
        gate[at, :] = g
        dz[at, :] = (cot[at, :].astype(F32) * g).astype(BF)
        return carry

    for i in range(nb):
        to_far(1, i).wait_recv()
        onward(1, i).start()
    lax.fori_loop(0, nb, gating, 0)
    for i in range(nb):
        to_other(1, i).wait_recv()
        onward(1, i).wait_recv()

    def back(j, carry):
        at = pl.ds(pl.multiple_of(j * order, order), order)
        dcolumn[j] = dot(block(1, j), dz[at, :], 0, 0).astype(BF)
        return carry

    lax.fori_loop(0, nb, back, 0)

    def pack_back(g, carry):
        at = pl.ds(pl.multiple_of(g * span, span), span)
        stack = jnp.concatenate([dcolumn[j, at] for j in range(nb)], axis=0)
        out = dot(mix8[...], stack)
        where = pl.ds(g * group, group)
        send2[0, where] = out[:rows4].reshape(group, 8, width).astype(BF)
        send2[1, where] = out[rows4:].reshape(group, 8, width).astype(BF)
        return carry

    lax.fori_loop(0, groups, pack_back, 0)
    for h in range(2):
        exchange(1, h, send2, land2)

    def near_own(f, q):
        return push(
            term.at[f, q, other], near.at[f, q, 0], rs_send.at[f, q, 0], rs_recv.at[f, q, 0], {"batch": other}
        )

    def near_far(f, q):
        return push(
            term.at[f, q, other_far], near.at[f, q, 1], rs_send.at[f, q, 1], rs_recv.at[f, q, 1], {"batch": other}
        )

    def across(f, q):
        return push(
            staged.at[f, q], away.at[f, q], rs_send.at[f, q, 2], rs_recv.at[f, q, 2], {"batch": far}
        )

    def middle(f, q):
        near_own(f, q).wait_recv()
        near_far(f, q).wait_recv()
        staged[f, q] = (term[f, q, far].astype(F32) + near[f, q, 1].astype(F32)).astype(BF)
        across(f, q).start()

    def finish(f, q, out):
        across(f, q).wait_recv()
        here = term[f, q, b].astype(F32) + near[f, q, 0].astype(F32)
        out[q] = (here + away[f, q].astype(F32)).astype(BF)

    for h in range(2):
        exchanged(0, h, send1, land1).wait_recv()

    def unpack(g, carry):
        where = pl.ds(g * group, group)
        halves = [land1[h, where].astype(F32).reshape(rows4, width).astype(BF) for h in range(2)]
        out = dot(mix8[...], jnp.concatenate(halves, axis=0), 0, 0).astype(BF)
        at = pl.ds(pl.multiple_of(g * span, span), span)
        for j in range(nb):
            column[j, at] = out[j * span : (j + 1) * span]
        return carry

    lax.fori_loop(0, groups, unpack, 0)

    def ahead(j, carry):
        at = pl.ds(pl.multiple_of(j * order, order), order)
        here = column[j]
        term[1, j] = dot(dz[at, :], here, 1, 1).astype(BF).reshape(4, part, order)
        near_own(1, j).start()
        near_far(1, j).start()
        z = dot(block(1, j), here)
        g = gate[at, :]
        dgate = cot[at, :].astype(F32) * z * g * (1.0 - g)
        high = dgate.astype(BF)
        low = (dgate - high.astype(F32)).astype(BF)
        spread[at, :] = dot(high, select[...], 1, 1) + dot(low, select[...], 1, 1)
        return carry

    lax.fori_loop(0, nb, ahead, 0)
    for q in range(nb):
        middle(1, q)
    for q in range(nb):
        finish(1, q, grad_second)

    for h in range(2):
        exchanged(1, h, send2, land2).wait_recv()

        def unpack_back(g, carry, h=h):
            piece = land2[h, pl.ds(g * group, group)].astype(F32).reshape(rows4, width).astype(BF)
            out = dot(mix4[...], piece, 0, 0).astype(BF)
            at = pl.ds(pl.multiple_of(g * span, span), span)
            regrouped[0, at] = out[:span]
            regrouped[1, at] = out[span:]
            return carry

        lax.fori_loop(0, groups, unpack_back, 0)

        def under(i2, carry, h=h):
            i = 2 * h + i2
            at = pl.ds(pl.multiple_of(i * order, order), order)
            dm = dot(pick_t[...], regrouped[i2]).astype(BF)
            dmixed[i2] = dm
            term[0, i] = dot(dm, tokens[at, :], 1, 1).astype(BF).reshape(4, part, order)
            near_own(0, i).start()
            near_far(0, i).start()
            return carry

        lax.fori_loop(0, 2, under, 0)

        def down(i2, carry, h=h):
            i = 2 * h + i2
            at = pl.ds(pl.multiple_of(i * order, order), order)
            inner = dot(block(0, i), dmixed[i2], 0, 0)
            grad_tokens[at, :] = (inner + spread[at, :]).astype(BF)
            middle(0, i)
            return carry

        lax.fori_loop(0, 2, down, 0)
    for q in range(nb):
        finish(0, q, grad_first)

    for f in range(2):
        for i in range(nb):
            to_far(f, i).wait_send()
            to_other(f, i).wait_send()
            onward(f, i).wait_send()
            near_own(f, i).wait_send()
            near_far(f, i).wait_send()
            across(f, i).wait_send()
    for h in range(2):
        exchanged(0, h, send1, land1).wait_send()
        exchanged(1, h, send2, land2).wait_send()


def solution(mesh):
    n = mesh.shape["seq"]

    def shards(tokens, cotangent, first_factor, second_factor, gate_source, alternate):
        nb, part, order = first_factor.shape
        rows, width = tokens.shape[1:]
        group = min(16, n)
        vmem = pltpu.VMEM
        out = pl.pallas_call(
            functools.partial(kernel, n),
            out_shape=[
                jax.ShapeDtypeStruct((rows, width), BF),
                jax.ShapeDtypeStruct((nb, part, order), BF),
                jax.ShapeDtypeStruct((nb, part, order), BF),
            ],
            in_specs=[pl.BlockSpec(memory_space=vmem)] * 6,
            out_specs=[pl.BlockSpec(memory_space=vmem)] * 3,
            scratch_shapes=[
                vmem((2, nb, 4, part, order), BF),
                vmem((width, width), BF),
                vmem((rows, width), F32),
                vmem((rows, width), BF),
                vmem((rows, width), F32),
                vmem((order, order), BF),
                vmem((order, order), BF),
                vmem((group * 8, group * 8), BF),
                vmem((group * 16, group * 16), BF),
                vmem((nb, order, width), BF),
                vmem((2, n, 8, width), BF),
                vmem((2, n, 8, width), BF),
                vmem((2, n, 8, width), BF),
                vmem((2, n, 8, width), BF),
                vmem((2, order, width), BF),
                vmem((nb, order, width), BF),
                vmem((2, order, width), BF),
                vmem((2, nb, 4, part, order), BF),
                vmem((2, nb, 2, part, order), BF),
                vmem((2, nb, part, order), BF),
                vmem((2, nb, part, order), BF),
                pltpu.SemaphoreType.DMA((2, nb, 3)),
                pltpu.SemaphoreType.DMA((2, nb, 3)),
                pltpu.SemaphoreType.DMA((2, 2)),
                pltpu.SemaphoreType.DMA((2, 2)),
                pltpu.SemaphoreType.DMA((2, nb, 3)),
                pltpu.SemaphoreType.DMA((2, nb, 3)),
            ],
            compiler_params=pltpu.CompilerParams(
                collective_id=0, has_side_effects=True, vmem_limit_bytes=56 << 20
            ),
        )(
            tokens[0],
            cotangent[0],
            first_factor,
            second_factor,
            gate_source.reshape(1, -1),
            alternate.reshape(1, -1),
        )
        return out[0][None], out[1], out[2]

    in_specs = (
        P("batch", "seq", None),
        P("batch", "seq", None),
        P("seq", "batch", None),
        P("seq", "batch", None),
        P(),
        P(),
    )
    out_specs = (P("batch", "seq", None), P("seq", "batch", None), P("seq", "batch", None))
    return jax.shard_map(shards, mesh=mesh, in_specs=in_specs, out_specs=out_specs, check_vma=False)
```

```python
import functools

import jax
import jax.numpy as jnp
from jax import lax
from jax.experimental import pallas as pl
from jax.experimental.pallas import tpu as pltpu
from jax.sharding import PartitionSpec as P

MESH = pl.DeviceIdType.MESH
BF = jnp.bfloat16
F32 = jnp.float32


def push(src, dst, send_sem, recv_sem, device):
    return pltpu.make_async_remote_copy(
        src_ref=src,
        dst_ref=dst,
        send_sem=send_sem,
        recv_sem=recv_sem,
        device_id=device,
        device_id_type=MESH,
    )


def dot(a, b, da=1, db=0):
    return lax.dot_general(a, b, (((da,), (db,)), ((), ())), preferred_element_type=F32)


def kernel(
    n,
    tokens_in,
    cot_in,
    first,
    second,
    source,
    alt,
    grad_tokens,
    grad_first,
    grad_second,
    tokens,
    cot,
    full,
    select,
    gate,
    dz,
    spread,
    pick,
    pick_t,
    mix4,
    mix8,
    mixq,
    column,
    send1,
    land1,
    send1q,
    land1q,
    send2,
    land2,
    send2q,
    land2q,
    regrouped,
    dcolumn,
    dmixed,
    term,
    near,
    staged,
    away,
    ag_send,
    ag_recv,
    a2a_send,
    a2a_recv,
    rs_send,
    rs_recv,
    in_sem,
):
    order = alt.shape[1]
    width = tokens.shape[1]
    nb = first.shape[0]
    part = first.shape[1]
    group = min(16, n)
    groups = n // group
    span = group * nb
    s = lax.axis_index("seq")
    b = lax.axis_index("batch")
    other = b + 1 - 2 * lax.rem(b, 2)
    far = lax.rem(b + 2, 4)
    other_far = lax.rem(other + 2, 4)
    shards = (first, second)

    barrier = pltpu.get_barrier_semaphore()
    for peer in (other, far):
        pl.semaphore_signal(barrier, inc=1, device_id={"batch": peer}, device_id_type=MESH)

    def greet(r, carry):
        pl.semaphore_signal(
            barrier, inc=1, device_id={"seq": lax.rem(s + r, n)}, device_id_type=MESH
        )
        return carry

    lax.fori_loop(1, n, greet, 0)

    loads = [pltpu.make_async_copy(tokens_in, tokens, in_sem.at[0])]
    for f in range(2):
        loads.append(pltpu.make_async_copy(shards[f], full.at[f, :, b], in_sem.at[1 + f]))
    loads.append(pltpu.make_async_copy(cot_in, cot, in_sem.at[3]))
    for load in loads:
        load.start()

    pl.semaphore_wait(barrier, n + 1)

    def to_far(f, i):
        return push(
            shards[f].at[i], full.at[f, i, b], ag_send.at[f, i, 0], ag_recv.at[f, i, 0], {"batch": far}
        )

    def to_other(f, i):
        return push(
            shards[f].at[i], full.at[f, i, b], ag_send.at[f, i, 1], ag_recv.at[f, i, 1], {"batch": other}
        )

    def onward(f, i):
        return push(
            full.at[f, i, far], full.at[f, i, far], ag_send.at[f, i, 2], ag_recv.at[f, i, 2], {"batch": other}
        )

    for f in range(2):
        for i in range(nb):
            to_far(f, i).start()
            to_other(f, i).start()

    row = lax.broadcasted_iota(jnp.int32, (order, order), 0)
    hit = (row == alt[...]).astype(F32)
    pick_t[...] = hit.astype(BF)
    pick[...] = hit.T.astype(BF)
    select[...] = (
        lax.broadcasted_iota(jnp.int32, (width, width), 0) == source[...]
    ).astype(F32).astype(BF)
    rows4 = group * 8
    r4 = lax.broadcasted_iota(jnp.int32, (rows4, rows4), 0)
    c4 = lax.broadcasted_iota(jnp.int32, (rows4, rows4), 1)
    want = ((r4 // 4) % 2) * span + (r4 // 8) * 4 + r4 % 4
    mix4[...] = (want == c4).astype(F32).astype(BF)
    rows8 = group * 16
    r8 = lax.broadcasted_iota(jnp.int32, (rows8, rows8), 0)
    c8 = lax.broadcasted_iota(jnp.int32, (rows8, rows8), 1)
    want = (r8 % 4) * span + ((r8 // 8) % group) * 4 + (r8 // rows4) * 2 + (r8 // 4) % 2
    mix8[...] = (want == c8).astype(F32).astype(BF)
    rq = lax.broadcasted_iota(jnp.int32, (rows8, 2 * rows8), 0)
    cq = lax.broadcasted_iota(jnp.int32, (rows8, 2 * rows8), 1)
    want = ((rq // 4) % 2) * rows8 + (rq % 4) * span + ((rq // 8) % group) * 4 + rq // rows4
    for h in range(2):
        mixq[h] = (want + 2 * h == cq).astype(F32).astype(BF)

    loads[0].wait()
    loads[1].wait()

    def block(f, i):
        return full[f, i].reshape(order, order)

    def exchange(k, buf, land):
        def go(r, carry):
            p = lax.rem(s + r, n)
            push(buf.at[p], land.at[s], a2a_send.at[k], a2a_recv.at[k], {"seq": p}).start()
            return carry

        lax.fori_loop(1, n, go, 0)
        land[s] = buf[s]

    def exchanged(k, buf, land):
        rest = pl.ds(0, n - 1)
        return push(
            buf.at[rest], land.at[rest], a2a_send.at[k], a2a_recv.at[k], {"seq": lax.rem(s + 1, n)}
        )

    lanes = width // 2

    def apply(i, slot):
        to_other(0, i).wait_recv()
        onward(0, i).wait_recv()
        mixed = dot(block(0, i), tokens[i * order : (i + 1) * order, :]).astype(BF)
        regrouped[slot] = dot(pick[...], mixed).astype(BF)

    for i in range(2):
        to_far(0, i).wait_recv()
        onward(0, i).start()
        apply(i, i)

        def pack_one(g, carry, i=i):
            at = pl.ds(pl.multiple_of(g * span, span), span)
            own = regrouped[i, at]
            stack = jnp.concatenate([own[:, :lanes], own[:, lanes:]], axis=0)
            out = dot(mix4[...], stack)
            send1q[i, pl.ds(g * group, group)] = out.reshape(group, 8, lanes).astype(BF)
            return carry

        lax.fori_loop(0, groups, pack_one, 0)
        exchange(i, send1q.at[i], land1q.at[i])
    for i in (2, 3):
        to_far(0, i).wait_recv()
        onward(0, i).start()
    for i in (2, 3):
        apply(i, i - 2)

    def pack(g, carry):
        at = pl.ds(pl.multiple_of(g * span, span), span)
        stack = jnp.concatenate([regrouped[0, at], regrouped[1, at]], axis=0)
        out = dot(mix4[...], stack)
        send1[pl.ds(g * group, group)] = out.reshape(group, 8, width).astype(BF)
        return carry

    lax.fori_loop(0, groups, pack, 0)
    exchange(2, send1, land1)

    def gating(q, carry):
        at = pl.ds(pl.multiple_of(q * order, order), order)
        g = jax.nn.sigmoid(dot(tokens[at, :], select[...]))
        gate[at, :] = g
        dz[at, :] = (cot[at, :].astype(F32) * g).astype(BF)
        return carry

    for i in range(nb):
        to_far(1, i).wait_recv()
        onward(1, i).start()
    loads[3].wait()
    lax.fori_loop(0, nb, gating, 0)
    loads[2].wait()
    for i in range(nb):
        to_other(1, i).wait_recv()
        onward(1, i).wait_recv()

    def back(j, carry):
        at = pl.ds(pl.multiple_of(j * order, order), order)
        dcolumn[j] = dot(block(1, j), dz[at, :], 0, 0).astype(BF)
        return carry

    lax.fori_loop(0, nb, back, 0)

    def pack_back(g, carry):
        at = pl.ds(pl.multiple_of(g * span, span), span)
        stack = jnp.concatenate([dcolumn[j, at] for j in range(nb)], axis=0)
        where = pl.ds(g * group, group)
        out = dot(mix8[:rows4], stack)
        send2[where] = out.reshape(group, 8, width).astype(BF)
        halves = jnp.concatenate([stack[:, :lanes], stack[:, lanes:]], axis=0)
        out = dot(mixq[1], halves)
        send2q[0, where] = out[:rows4].reshape(group, 8, lanes).astype(BF)
        send2q[1, where] = out[rows4:].reshape(group, 8, lanes).astype(BF)
        return carry

    lax.fori_loop(0, groups, pack_back, 0)
    exchange(3, send2, land2)
    for q in range(2):
        exchange(4 + q, send2q.at[q], land2q.at[q])

    def near_own(f, q):
        return push(
            term.at[f, q, other], near.at[f, q, 0], rs_send.at[f, q, 0], rs_recv.at[f, q, 0], {"batch": other}
        )

    def near_far(f, q):
        return push(
            term.at[f, q, other_far], near.at[f, q, 1], rs_send.at[f, q, 1], rs_recv.at[f, q, 1], {"batch": other}
        )

    def across(f, q):
        return push(
            staged.at[f, q], away.at[f, q], rs_send.at[f, q, 2], rs_recv.at[f, q, 2], {"batch": far}
        )

    def middle(f, q):
        near_own(f, q).wait_recv()
        near_far(f, q).wait_recv()
        staged[f, q] = (term[f, q, far].astype(F32) + near[f, q, 1].astype(F32)).astype(BF)
        across(f, q).start()

    def finish(f, q, out):
        across(f, q).wait_recv()
        here = term[f, q, b].astype(F32) + near[f, q, 0].astype(F32)
        out[q] = (here + away[f, q].astype(F32)).astype(BF)

    for q in range(2):
        exchanged(q, send1q.at[q], land1q.at[q]).wait_recv()
    exchanged(2, send1, land1).wait_recv()

    def unpack(g, carry):
        where = pl.ds(g * group, group)
        ones = [land1q[q, where].astype(F32).reshape(rows4, lanes).astype(BF) for q in range(2)]
        split = dot(mixq[0], jnp.concatenate(ones, axis=0), 0, 0)
        pair = land1[where].astype(F32).reshape(rows4, width).astype(BF)
        out = dot(mix8[rows4:], pair, 0, 0)
        out = (out + jnp.concatenate([split[:rows8], split[rows8:]], axis=1)).astype(BF)
        at = pl.ds(pl.multiple_of(g * span, span), span)
        for j in range(nb):
            column[j, at] = out[j * span : (j + 1) * span]
        return carry

    lax.fori_loop(0, groups, unpack, 0)

    def ahead(j, carry):
        at = pl.ds(pl.multiple_of(j * order, order), order)
        here = column[j]
        term[1, j] = dot(dz[at, :], here, 1, 1).astype(BF).reshape(4, part, order)
        near_own(1, j).start()
        near_far(1, j).start()
        z = dot(block(1, j), here)
        g = gate[at, :]
        dgate = cot[at, :].astype(F32) * z * g * (1.0 - g)
        high = dgate.astype(BF)
        low = (dgate - high.astype(F32)).astype(BF)
        spread[at, :] = dot(high, select[...], 1, 1) + dot(low, select[...], 1, 1)
        return carry

    lax.fori_loop(0, nb, ahead, 0)
    for q in range(nb):
        middle(1, q)
    for q in range(nb):
        finish(1, q, grad_second)

    def under(i, slot):
        at = pl.ds(i * order, order)
        dm = dot(pick_t[...], regrouped[slot]).astype(BF)
        dmixed[slot] = dm
        term[0, i] = dot(dm, tokens[at, :], 1, 1).astype(BF).reshape(4, part, order)
        near_own(0, i).start()
        near_far(0, i).start()

    def down(i, slot):
        at = pl.ds(i * order, order)
        inner = dot(block(0, i), dmixed[slot], 0, 0)
        grad_tokens[at, :] = (inner + spread[at, :]).astype(BF)
        middle(0, i)

    exchanged(3, send2, land2).wait_recv()

    def unpack_back(g, carry):
        piece = land2[pl.ds(g * group, group)].astype(F32).reshape(rows4, width).astype(BF)
        out = dot(mix4[...], piece, 0, 0).astype(BF)
        at = pl.ds(pl.multiple_of(g * span, span), span)
        regrouped[0, at] = out[:span]
        regrouped[1, at] = out[span:]
        return carry

    lax.fori_loop(0, groups, unpack_back, 0)
    for i in range(2):
        under(i, i)
    for i in range(2):
        down(i, i)
    for q in range(2):
        exchanged(4 + q, send2q.at[q], land2q.at[q]).wait_recv()

        def unpack_one(g, carry, q=q):
            piece = land2q[q, pl.ds(g * group, group)].astype(F32).reshape(rows4, lanes).astype(BF)
            out = dot(mix4[...], piece, 0, 0).astype(BF)
            at = pl.ds(pl.multiple_of(g * span, span), span)
            regrouped[q, at] = jnp.concatenate([out[:span], out[span:]], axis=1)
            return carry

        lax.fori_loop(0, groups, unpack_one, 0)
        under(2 + q, q)
        down(2 + q, q)
    for q in range(nb):
        finish(0, q, grad_first)

    for f in range(2):
        for i in range(nb):
            to_far(f, i).wait_send()
            to_other(f, i).wait_send()
            onward(f, i).wait_send()
            near_own(f, i).wait_send()
            near_far(f, i).wait_send()
            across(f, i).wait_send()
    for q in range(2):
        exchanged(q, send1q.at[q], land1q.at[q]).wait_send()
        exchanged(4 + q, send2q.at[q], land2q.at[q]).wait_send()
    exchanged(2, send1, land1).wait_send()
    exchanged(3, send2, land2).wait_send()


def hand_over(a, b, c, a_out, b_out, c_out):
    a_out[...] = a[...]
    b_out[...] = b[...]
    c_out[...] = c[...]


def solution(mesh):
    n = mesh.shape["seq"]

    def shards(tokens, cotangent, first_factor, second_factor, gate_source, alternate):
        nb, part, order = first_factor.shape
        rows, width = tokens.shape[1:]
        group = min(16, n)
        vmem = pltpu.VMEM
        out = pl.pallas_call(
            functools.partial(kernel, n),
            out_shape=[
                jax.ShapeDtypeStruct((rows, width), BF),
                jax.ShapeDtypeStruct((nb, part, order), BF),
                jax.ShapeDtypeStruct((nb, part, order), BF),
            ],
            in_specs=[pl.BlockSpec(memory_space=pl.ANY)] * 4
            + [pl.BlockSpec(memory_space=vmem)] * 2,
            out_specs=[pl.BlockSpec(memory_space=vmem)] * 3,
            scratch_shapes=[
                vmem((rows, width), BF),
                vmem((rows, width), BF),
                vmem((2, nb, 4, part, order), BF),
                vmem((width, width), BF),
                vmem((rows, width), F32),
                vmem((rows, width), BF),
                vmem((rows, width), F32),
                vmem((order, order), BF),
                vmem((order, order), BF),
                vmem((group * 8, group * 8), BF),
                vmem((group * 16, group * 16), BF),
                vmem((2, group * 16, group * 32), BF),
                vmem((nb, order, width), BF),
                vmem((n, 8, width), BF),
                vmem((n, 8, width), BF),
                vmem((2, n, 8, width // 2), BF),
                vmem((2, n, 8, width // 2), BF),
                vmem((n, 8, width), BF),
                vmem((n, 8, width), BF),
                vmem((2, n, 8, width // 2), BF),
                vmem((2, n, 8, width // 2), BF),
                vmem((2, order, width), BF),
                vmem((nb, order, width), BF),
                vmem((2, order, width), BF),
                vmem((2, nb, 4, part, order), BF),
                vmem((2, nb, 2, part, order), BF),
                vmem((2, nb, part, order), BF),
                vmem((2, nb, part, order), BF),
                pltpu.SemaphoreType.DMA((2, nb, 3)),
                pltpu.SemaphoreType.DMA((2, nb, 3)),
                pltpu.SemaphoreType.DMA((6,)),
                pltpu.SemaphoreType.DMA((6,)),
                pltpu.SemaphoreType.DMA((2, nb, 3)),
                pltpu.SemaphoreType.DMA((2, nb, 3)),
                pltpu.SemaphoreType.DMA((4,)),
            ],
            compiler_params=pltpu.CompilerParams(
                collective_id=0, has_side_effects=True, vmem_limit_bytes=56 << 20
            ),
        )(
            tokens[0],
            cotangent[0],
            first_factor,
            second_factor,
            gate_source.reshape(1, -1),
            alternate.reshape(1, -1),
        )
        out = pl.pallas_call(
            hand_over,
            out_shape=[jax.ShapeDtypeStruct(o.shape, o.dtype) for o in out],
            in_specs=[pl.BlockSpec(memory_space=vmem)] * 3,
            out_specs=[pl.BlockSpec(memory_space=vmem)] * 3,
        )(*out)
        return out[0][None], out[1], out[2]

    in_specs = (
        P("batch", "seq", None),
        P("batch", "seq", None),
        P("seq", "batch", None),
        P("seq", "batch", None),
        P(),
        P(),
    )
    out_specs = (P("batch", "seq", None), P("seq", "batch", None), P("seq", "batch", None))
    return jax.shard_map(shards, mesh=mesh, in_specs=in_specs, out_specs=out_specs, check_vma=False)
```

```python
import functools

import jax
import jax.numpy as jnp
from jax import lax
from jax.experimental import pallas as pl
from jax.experimental.pallas import tpu as pltpu
from jax.sharding import PartitionSpec as P

MESH = pl.DeviceIdType.MESH
BF = jnp.bfloat16
F32 = jnp.float32


def push(src, dst, send_sem, recv_sem, device):
    return pltpu.make_async_remote_copy(
        src_ref=src,
        dst_ref=dst,
        send_sem=send_sem,
        recv_sem=recv_sem,
        device_id=device,
        device_id_type=MESH,
    )


def dot(a, b, da=1, db=0):
    return lax.dot_general(a, b, (((da,), (db,)), ((), ())), preferred_element_type=F32)


def kernel(
    n,
    tokens_in,
    cot_in,
    first,
    second,
    source,
    alt,
    grad_tokens,
    grad_first,
    grad_second,
    tokens,
    cot,
    full,
    select,
    gate,
    dz,
    spread,
    pick,
    pick_t,
    mix4,
    mix8,
    mixq,
    column,
    send1,
    land1,
    send1q,
    land1q,
    send2,
    land2,
    send2q,
    land2q,
    regrouped,
    dcolumn,
    dmixed,
    term,
    near,
    staged,
    away,
    ag_send,
    ag_recv,
    a2a_send,
    a2a_recv,
    rs_send,
    rs_recv,
    in_sem,
):
    order = alt.shape[1]
    width = tokens.shape[1]
    nb = first.shape[0]
    part = first.shape[1]
    group = min(16, n)
    groups = n // group
    span = group * nb
    s = lax.axis_index("seq")
    b = lax.axis_index("batch")
    other = b + 1 - 2 * lax.rem(b, 2)
    far = lax.rem(b + 2, 4)
    other_far = lax.rem(other + 2, 4)
    shards = (first, second)

    barrier = pltpu.get_barrier_semaphore()
    for peer in (other, far):
        pl.semaphore_signal(barrier, inc=1, device_id={"batch": peer}, device_id_type=MESH)

    def greet(r, carry):
        pl.semaphore_signal(
            barrier, inc=1, device_id={"seq": lax.rem(s + r, n)}, device_id_type=MESH
        )
        return carry

    lax.fori_loop(1, n, greet, 0)

    loads = [pltpu.make_async_copy(tokens_in, tokens, in_sem.at[0])]
    for f in range(2):
        loads.append(pltpu.make_async_copy(shards[f], full.at[f, :, b], in_sem.at[1 + f]))
    loads.append(pltpu.make_async_copy(cot_in, cot, in_sem.at[3]))
    for load in loads:
        load.start()

    pl.semaphore_wait(barrier, n + 1)

    def to_far(f, i):
        return push(
            shards[f].at[i], full.at[f, i, b], ag_send.at[f, i, 0], ag_recv.at[f, i, 0], {"batch": far}
        )

    def to_other(f, i):
        return push(
            shards[f].at[i], full.at[f, i, b], ag_send.at[f, i, 1], ag_recv.at[f, i, 1], {"batch": other}
        )

    def onward(f, i):
        return push(
            full.at[f, i, far], full.at[f, i, far], ag_send.at[f, i, 2], ag_recv.at[f, i, 2], {"batch": other}
        )

    for f in range(2):
        for i in range(nb):
            to_far(f, i).start()
            to_other(f, i).start()

    row = lax.broadcasted_iota(jnp.int32, (order, order), 0)
    hit = (row == alt[...]).astype(F32)
    pick_t[...] = hit.astype(BF)
    pick[...] = hit.T.astype(BF)
    select[...] = (
        lax.broadcasted_iota(jnp.int32, (width, width), 0) == source[...]
    ).astype(F32).astype(BF)
    rows4 = group * 8
    r4 = lax.broadcasted_iota(jnp.int32, (rows4, rows4), 0)
    c4 = lax.broadcasted_iota(jnp.int32, (rows4, rows4), 1)
    want = ((r4 // 4) % 2) * span + (r4 // 8) * 4 + r4 % 4
    mix4[...] = (want == c4).astype(F32).astype(BF)
    rows8 = group * 16
    r8 = lax.broadcasted_iota(jnp.int32, (rows8, rows8), 0)
    c8 = lax.broadcasted_iota(jnp.int32, (rows8, rows8), 1)
    want = (r8 % 4) * span + ((r8 // 8) % group) * 4 + (r8 // rows4) * 2 + (r8 // 4) % 2
    mix8[...] = (want == c8).astype(F32).astype(BF)
    rq = lax.broadcasted_iota(jnp.int32, (rows8, 2 * rows8), 0)
    cq = lax.broadcasted_iota(jnp.int32, (rows8, 2 * rows8), 1)
    want = ((rq // 4) % 2) * rows8 + (rq % 4) * span + ((rq // 8) % group) * 4 + rq // rows4
    for h in range(2):
        mixq[h] = (want + 2 * h == cq).astype(F32).astype(BF)

    loads[0].wait()
    loads[1].wait()

    def block(f, i):
        return full[f, i].reshape(order, order)

    def exchange(k, buf, land):
        def go(r, carry):
            p = lax.rem(s + r, n)
            push(buf.at[p], land.at[s], a2a_send.at[k], a2a_recv.at[k], {"seq": p}).start()
            return carry

        lax.fori_loop(1, n, go, 0)
        land[s] = buf[s]

    def exchanged(k, buf, land):
        rest = pl.ds(0, n - 1)
        return push(
            buf.at[rest], land.at[rest], a2a_send.at[k], a2a_recv.at[k], {"seq": lax.rem(s + 1, n)}
        )

    lanes = width // 2

    def apply(i, slot):
        to_other(0, i).wait_recv()
        onward(0, i).wait_recv()
        mixed = dot(block(0, i), tokens[i * order : (i + 1) * order, :]).astype(BF)
        regrouped[slot] = dot(pick[...], mixed).astype(BF)

    for i in range(2):
        to_far(0, i).wait_recv()
        onward(0, i).start()
        apply(i, i)

        def pack_one(g, carry, i=i):
            at = pl.ds(pl.multiple_of(g * span, span), span)
            own = regrouped[i, at]
            stack = jnp.concatenate([own[:, :lanes], own[:, lanes:]], axis=0)
            out = dot(mix4[...], stack)
            send1q[i, pl.ds(g * group, group)] = out.reshape(group, 8, lanes).astype(BF)
            return carry

        lax.fori_loop(0, groups, pack_one, 0, unroll=True)
        exchange(i, send1q.at[i], land1q.at[i])
    for i in (2, 3):
        to_far(0, i).wait_recv()
        onward(0, i).start()
    for i in (2, 3):
        apply(i, i - 2)

    def pack(g, carry):
        at = pl.ds(pl.multiple_of(g * span, span), span)
        stack = jnp.concatenate([regrouped[0, at], regrouped[1, at]], axis=0)
        out = dot(mix4[...], stack)
        send1[pl.ds(g * group, group)] = out.reshape(group, 8, width).astype(BF)
        return carry

    lax.fori_loop(0, groups, pack, 0)
    exchange(2, send1, land1)

    def gating(q, carry):
        at = pl.ds(pl.multiple_of(q * order, order), order)
        g = jax.nn.sigmoid(dot(tokens[at, :], select[...]))
        gate[at, :] = g
        dz[at, :] = (cot[at, :].astype(F32) * g).astype(BF)
        return carry

    for i in range(nb):
        to_far(1, i).wait_recv()
        onward(1, i).start()
    loads[3].wait()
    lax.fori_loop(0, nb, gating, 0)
    loads[2].wait()
    for i in range(nb):
        to_other(1, i).wait_recv()
        onward(1, i).wait_recv()

    def back(j, carry):
        at = pl.ds(pl.multiple_of(j * order, order), order)
        dcolumn[j] = dot(block(1, j), dz[at, :], 0, 0).astype(BF)
        return carry

    lax.fori_loop(0, nb, back, 0)

    def pack_back(g, carry):
        at = pl.ds(pl.multiple_of(g * span, span), span)
        stack = jnp.concatenate([dcolumn[j, at] for j in range(nb)], axis=0)
        where = pl.ds(g * group, group)
        out = dot(mix8[:rows4], stack)
        send2[where] = out.reshape(group, 8, width).astype(BF)
        halves = jnp.concatenate([stack[:, :lanes], stack[:, lanes:]], axis=0)
        out = dot(mixq[1], halves)
        send2q[0, where] = out[:rows4].reshape(group, 8, lanes).astype(BF)
        send2q[1, where] = out[rows4:].reshape(group, 8, lanes).astype(BF)
        return carry

    lax.fori_loop(0, groups, pack_back, 0)
    exchange(3, send2, land2)
    for q in range(2):
        exchange(4 + q, send2q.at[q], land2q.at[q])

    def near_own(f, q):
        return push(
            term.at[f, q, other], near.at[f, q, 0], rs_send.at[f, q, 0], rs_recv.at[f, q, 0], {"batch": other}
        )

    def near_far(f, q):
        return push(
            term.at[f, q, other_far], near.at[f, q, 1], rs_send.at[f, q, 1], rs_recv.at[f, q, 1], {"batch": other}
        )

    def across(f, q):
        return push(
            staged.at[f, q], away.at[f, q], rs_send.at[f, q, 2], rs_recv.at[f, q, 2], {"batch": far}
        )

    def middle(f, q):
        near_own(f, q).wait_recv()
        near_far(f, q).wait_recv()
        staged[f, q] = (term[f, q, far].astype(F32) + near[f, q, 1].astype(F32)).astype(BF)
        across(f, q).start()

    def finish(f, q, out):
        across(f, q).wait_recv()
        here = term[f, q, b].astype(F32) + near[f, q, 0].astype(F32)
        out[q] = (here + away[f, q].astype(F32)).astype(BF)

    for q in range(2):
        exchanged(q, send1q.at[q], land1q.at[q]).wait_recv()
    exchanged(2, send1, land1).wait_recv()

    def unpack(g, carry):
        where = pl.ds(g * group, group)
        ones = [land1q[q, where].astype(F32).reshape(rows4, lanes).astype(BF) for q in range(2)]
        split = dot(mixq[0], jnp.concatenate(ones, axis=0), 0, 0)
        pair = land1[where].astype(F32).reshape(rows4, width).astype(BF)
        out = dot(mix8[rows4:], pair, 0, 0)
        out = (out + jnp.concatenate([split[:rows8], split[rows8:]], axis=1)).astype(BF)
        at = pl.ds(pl.multiple_of(g * span, span), span)
        for j in range(nb):
            column[j, at] = out[j * span : (j + 1) * span]
        return carry

    lax.fori_loop(0, groups, unpack, 0)

    def ahead(j, carry):
        at = pl.ds(pl.multiple_of(j * order, order), order)
        here = column[j]
        term[1, j] = dot(dz[at, :], here, 1, 1).astype(BF).reshape(4, part, order)
        near_own(1, j).start()
        near_far(1, j).start()
        z = dot(block(1, j), here)
        g = gate[at, :]
        dgate = cot[at, :].astype(F32) * z * g * (1.0 - g)
        high = dgate.astype(BF)
        low = (dgate - high.astype(F32)).astype(BF)
        spread[at, :] = dot(high, select[...], 1, 1) + dot(low, select[...], 1, 1)
        return carry

    lax.fori_loop(0, nb, ahead, 0)
    for q in range(nb):
        middle(1, q)
    for q in range(nb):
        finish(1, q, grad_second)

    def under(i, slot):
        at = pl.ds(i * order, order)
        dm = dot(pick_t[...], regrouped[slot]).astype(BF)
        dmixed[slot] = dm
        term[0, i] = dot(dm, tokens[at, :], 1, 1).astype(BF).reshape(4, part, order)
        near_own(0, i).start()
        near_far(0, i).start()

    def down(i, slot):
        at = pl.ds(i * order, order)
        inner = dot(block(0, i), dmixed[slot], 0, 0)
        grad_tokens[at, :] = (inner + spread[at, :]).astype(BF)
        middle(0, i)

    exchanged(3, send2, land2).wait_recv()

    def unpack_back(g, carry):
        piece = land2[pl.ds(g * group, group)].astype(F32).reshape(rows4, width).astype(BF)
        out = dot(mix4[...], piece, 0, 0).astype(BF)
        at = pl.ds(pl.multiple_of(g * span, span), span)
        regrouped[0, at] = out[:span]
        regrouped[1, at] = out[span:]
        return carry

    lax.fori_loop(0, groups, unpack_back, 0)
    for i in range(2):
        under(i, i)
    for i in range(2):
        down(i, i)
    for q in range(2):
        if q == 1:
            finish(0, 0, grad_first)
            finish(0, 1, grad_first)
        exchanged(4 + q, send2q.at[q], land2q.at[q]).wait_recv()

        def unpack_one(g, carry, q=q):
            piece = land2q[q, pl.ds(g * group, group)].astype(F32).reshape(rows4, lanes).astype(BF)
            out = dot(mix4[...], piece, 0, 0).astype(BF)
            at = pl.ds(pl.multiple_of(g * span, span), span)
            regrouped[q, at] = jnp.concatenate([out[:span], out[span:]], axis=1)
            return carry

        lax.fori_loop(0, groups, unpack_one, 0, unroll=True)
        under(2 + q, q)
        down(2 + q, q)
    for q in range(2, nb):
        finish(0, q, grad_first)

    for f in range(2):
        for i in range(nb):
            to_far(f, i).wait_send()
            to_other(f, i).wait_send()
            onward(f, i).wait_send()
            near_own(f, i).wait_send()
            near_far(f, i).wait_send()
            across(f, i).wait_send()
    for q in range(2):
        exchanged(q, send1q.at[q], land1q.at[q]).wait_send()
        exchanged(4 + q, send2q.at[q], land2q.at[q]).wait_send()
    exchanged(2, send1, land1).wait_send()
    exchanged(3, send2, land2).wait_send()


def hand_over(a, b, c, a_out, b_out, c_out, a_held, b_held, c_held, got, sent):
    helds = (a_held, b_held, c_held)
    ins = [pltpu.make_async_copy(x, held, got.at[q]) for q, (x, held) in enumerate(zip((a, b, c), helds))]
    outs = [
        pltpu.make_async_copy(held, x, sent.at[q])
        for q, (x, held) in enumerate(zip((a_out, b_out, c_out), helds))
    ]
    for copy in ins:
        copy.start()
    for load, store in zip(ins, outs):
        load.wait()
        store.start()
    for copy in outs:
        copy.wait()


def solution(mesh):
    n = mesh.shape["seq"]

    def shards(tokens, cotangent, first_factor, second_factor, gate_source, alternate):
        nb, part, order = first_factor.shape
        rows, width = tokens.shape[1:]
        group = min(16, n)
        vmem = pltpu.VMEM
        out = pl.pallas_call(
            functools.partial(kernel, n),
            out_shape=[
                jax.ShapeDtypeStruct((rows, width), BF),
                jax.ShapeDtypeStruct((nb, part, order), BF),
                jax.ShapeDtypeStruct((nb, part, order), BF),
            ],
            in_specs=[pl.BlockSpec(memory_space=pl.ANY)] * 4
            + [pl.BlockSpec(memory_space=vmem)] * 2,
            out_specs=[pl.BlockSpec(memory_space=vmem)] * 3,
            scratch_shapes=[
                vmem((rows, width), BF),
                vmem((rows, width), BF),
                vmem((2, nb, 4, part, order), BF),
                vmem((width, width), BF),
                vmem((rows, width), F32),
                vmem((rows, width), BF),
                vmem((rows, width), F32),
                vmem((order, order), BF),
                vmem((order, order), BF),
                vmem((group * 8, group * 8), BF),
                vmem((group * 16, group * 16), BF),
                vmem((2, group * 16, group * 32), BF),
                vmem((nb, order, width), BF),
                vmem((n, 8, width), BF),
                vmem((n, 8, width), BF),
                vmem((2, n, 8, width // 2), BF),
                vmem((2, n, 8, width // 2), BF),
                vmem((n, 8, width), BF),
                vmem((n, 8, width), BF),
                vmem((2, n, 8, width // 2), BF),
                vmem((2, n, 8, width // 2), BF),
                vmem((2, order, width), BF),
                vmem((nb, order, width), BF),
                vmem((2, order, width), BF),
                vmem((2, nb, 4, part, order), BF),
                vmem((2, nb, 2, part, order), BF),
                vmem((2, nb, part, order), BF),
                vmem((2, nb, part, order), BF),
                pltpu.SemaphoreType.DMA((2, nb, 3)),
                pltpu.SemaphoreType.DMA((2, nb, 3)),
                pltpu.SemaphoreType.DMA((6,)),
                pltpu.SemaphoreType.DMA((6,)),
                pltpu.SemaphoreType.DMA((2, nb, 3)),
                pltpu.SemaphoreType.DMA((2, nb, 3)),
                pltpu.SemaphoreType.DMA((4,)),
            ],
            compiler_params=pltpu.CompilerParams(
                collective_id=0, has_side_effects=True, vmem_limit_bytes=56 << 20
            ),
        )(
            tokens[0],
            cotangent[0],
            first_factor,
            second_factor,
            gate_source.reshape(1, -1),
            alternate.reshape(1, -1),
        )
        out = pl.pallas_call(
            hand_over,
            out_shape=[jax.ShapeDtypeStruct(o.shape, o.dtype) for o in out],
            in_specs=[pl.BlockSpec(memory_space=pl.ANY)] * 3,
            out_specs=[pl.BlockSpec(memory_space=pl.ANY)] * 3,
            scratch_shapes=[vmem(o.shape, o.dtype) for o in out]
            + [pltpu.SemaphoreType.DMA((3,)), pltpu.SemaphoreType.DMA((3,))],
            compiler_params=pltpu.CompilerParams(vmem_limit_bytes=56 << 20),
        )(*out)
        return out[0][None], out[1], out[2]

    in_specs = (
        P("batch", "seq", None),
        P("batch", "seq", None),
        P("seq", "batch", None),
        P("seq", "batch", None),
        P(),
        P(),
    )
    out_specs = (P("batch", "seq", None), P("seq", "batch", None), P("seq", "batch", None))
    return jax.shard_map(shards, mesh=mesh, in_specs=in_specs, out_specs=out_specs, check_vma=False)
```
